256 devices in a mesh: tm: 16 (over y, x), tile: 16 (over z, core).
Axes of the slice: x: 4, y: 4, z: 8, core: 2. Of those that a mesh axis runs over, the one named last changes fastest.
Arguments:
- latent: bfloat16 [64, 64, 32, 256], P('tm', 'tile'), may hold values from -6 to 6
- tile_rows: int32 [16], replicated, may hold values from 1 to 4, 32 in all
- kernel_one: bfloat16 [3, 3, 3, 256, 256], replicated, may hold values from -0.078125 to 0.078125
- bias_one: float32 [256], replicated, may hold values from -3 to 3
- kernel_two: bfloat16 [3, 3, 3, 256, 256], replicated, may hold values from -0.078125 to 0.078125
- bias_two: float32 [256], replicated, may hold values from -3 to 3
Outputs:
- frames_out: bfloat16 [64, 128, 64, 256], P('tm', 'tile')
The draws below stay inside these ranges and needn't reach their ends.
Inputs may be any that keep to these rules, and one draw needn't show every extreme that they name: `tile_rows`: each tile has 1 to 4 rows, they sum to 32, and some tile has exactly 4.
All inputs are finite; a program needn't handle non-finite values.
Results may differ from the reference program's by a relative error of at most 0.0031.
Values may be sent and summed in bfloat16 or wider, within the bound.
A program may use at most 64 MiB of HBM per device.

```python
import math
import jax
import jax.numpy as jnp
import numpy as np
from jax import lax

CHANNELS = 256
ROW_CAP = 4
LAT_COLS = 32
FRAMES = 64
TOTAL_ROWS = 32
N_TILE = 16


def block_levels(own_key, shape, split, least, top_value):
    loudness, own = 1.0, jax.random.fold_in(own_key, 6)
    for dim, parts in split:
        draws = jnp.exp(jax.random.uniform(jax.random.fold_in(own, dim), (parts,), jnp.float32, least / len(split), top_value / len(split)))
        loudness = loudness * jnp.repeat(draws, shape[dim] // parts).reshape([-1 if axis == dim else 1 for axis in range(len(shape))])
    return loudness


def profile(count, total, bound, skew):
    weights = [(1 << 20) // math.isqrt(grade ** skew) + 1 for grade in range(2, count + 1)]
    rest, counts = total - bound - (count - 1), [1] * (count - 1)
    while rest > 0:
        free = [i for i in range(count - 1) if counts[i] < bound]
        whole, budget = sum([weights[i] for i in free]), rest
        for i in free:
            extra = min(bound - counts[i], max(1, budget * weights[i] // whole), rest)
            counts[i] = counts[i] + extra
            rest = rest - extra
    return np.array([bound] + counts)


def uneven(key, count, total, limit, skew):
    if count == 2:
        one = jax.random.randint(key, (), max(1, total - limit), min(limit, total - 1) + 1)
        return jnp.stack([one, total - one])
    sizes = jnp.asarray(profile(count, total, limit, skew), jnp.int32)
    twos = (count - 1) // 2
    source_of, receiver = sizes[1:1 + 2 * twos:2], sizes[2:2 + 2 * twos:2]
    room = jnp.minimum(source_of - 1, limit - receiver)
    shifted = jax.random.randint(jax.random.fold_in(key, 1), (twos,), 0, 1 << 20) % (room + 1)
    sizes = sizes.at[1:1 + 2 * twos:2].set(source_of - shifted).at[2:2 + 2 * twos:2].set(receiver + shifted)
    return sizes[jax.random.permutation(jax.random.fold_in(key, 2), count)]


def centred(key, extent, deviation, limit, split=(), held_as=jnp.bfloat16):
    factor_of = block_levels(key, extent, split, -0.22, 0.18) if split else 1.0
    values = jax.random.normal(key, extent, jnp.float32) * deviation * factor_of
    return jnp.minimum(jnp.maximum(values, -limit), limit).astype(held_as)


def setup_inputs(seed: int = 0) -> dict:
    seeds = jax.random.split(jax.random.key(seed), 7)
    return {
        "latent": centred(seeds[0], (FRAMES, ROW_CAP * N_TILE, LAT_COLS, CHANNELS), 1.0, 6.0, ((0, 16), (1, 16))),
        "tile_rows": uneven(seeds[1], N_TILE, TOTAL_ROWS, ROW_CAP, 2).astype(jnp.int32),
        "kernel_one": centred(seeds[2], (3, 3, 3, CHANNELS, CHANNELS), (27 * CHANNELS) ** -0.5, 0.078125),
        "bias_one": centred(seeds[3], (CHANNELS,), 0.5, 3.0, (), jnp.float32),
        "kernel_two": centred(seeds[4], (3, 3, 3, CHANNELS, CHANNELS), (27 * CHANNELS) ** -0.5, 0.078125),
        "bias_two": centred(seeds[5], (CHANNELS,), 0.5, 3.0, (), jnp.float32),
    }


def convolve(field, kernel, bias):
    padded = jnp.concatenate([field[0:1], field[0:1], field], axis=0)
    padded = jnp.pad(padded, ((0, 0), (1, 1), (1, 1), (0, 0)))
    result = lax.conv_general_dilated(padded[None], kernel.astype(jnp.float32), (1, 1, 1), "VALID",
                                      dimension_numbers=("NDHWC", "DHWIO", "NDHWC"),
                                      precision=lax.Precision.HIGHEST)
    return result[0] + bias.astype(jnp.float32)


def reference(latent, tile_rows, kernel_one, bias_one, kernel_two, bias_two):
    lengths = tile_rows.astype(jnp.int32)
    starts = (jnp.cumsum(lengths) - lengths).astype(jnp.int32)
    rows_global = jnp.arange(TOTAL_ROWS, dtype=jnp.int32)
    owner = (jnp.sum((starts[None, :] <= rows_global[:, None]).astype(jnp.int32), axis=1) - 1).astype(jnp.int32)
    source = (owner * ROW_CAP + rows_global - jnp.take(starts, owner)).astype(jnp.int32)
    image = jnp.take(latent, source, axis=1)
    upsampled = jnp.repeat(jnp.repeat(image, 2, axis=1), 2, axis=2).astype(jnp.float32)
    hidden = jax.nn.silu(convolve(upsampled, kernel_one, bias_one)).astype(jnp.bfloat16)
    mixed = (convolve(hidden.astype(jnp.float32), kernel_two, bias_two) + upsampled).astype(jnp.bfloat16)
    slots = jnp.arange(2 * ROW_CAP * N_TILE, dtype=jnp.int32)
    owner_slot = (slots // (2 * ROW_CAP)).astype(jnp.int32)
    offset = (slots % (2 * ROW_CAP)).astype(jnp.int32)
    valid = offset < 2 * jnp.take(lengths, owner_slot)
    target = jnp.clip(2 * jnp.take(starts, owner_slot) + offset, 0, 2 * TOTAL_ROWS - 1).astype(jnp.int32)
    placed = jnp.take(mixed, target, axis=1)
    return jnp.where(valid[None, :, None, None], placed, jnp.zeros((), jnp.bfloat16))
```

```python
import functools

import jax
import jax.numpy as jnp
from jax import lax
from jax.experimental import pallas as pl
from jax.experimental.pallas import tpu as pltpu
from jax.sharding import PartitionSpec as P

MESH = pl.DeviceIdType.MESH
F32, BF16 = jnp.float32, jnp.bfloat16


def shifted(value, by, cols, keep):
    return jnp.where(keep, pltpu.roll(value, by % value.shape[0], axis=0), 0.0)


def spread(ext, hid, k, w1, half_bias, first, last, length, dims):
    cap, cols, ch = dims
    n = (cap + 1) * cols
    taps = jnp.concatenate([ext[k], ext[k + 1], ext[k + 2]], axis=1)
    upper, lower = taps[:n], taps[cols:]
    ends = jnp.concatenate([upper, lower], axis=1)
    side = lax.broadcasted_iota(jnp.int32, (n, ch), 0) % cols
    after_first, before_last = side != 0, side != cols - 1
    even_rows, odd_rows = [], []
    for q in range(3):
        outer = jnp.concatenate([w1[:, 0, q].reshape(3 * ch, ch), w1[:, 2, q].reshape(3 * ch, ch)], axis=0)
        shared = jnp.dot(ends, outer, preferred_element_type=F32)
        centre = jnp.dot(taps, w1[:, 1, q].reshape(3 * ch, ch), preferred_element_type=F32)
        even_rows.append(shared + centre[cols:])
        odd_rows.append(shared + centre[:n])
    slot = lax.broadcasted_iota(jnp.int32, (n, ch), 0) // cols
    keep_odd = jnp.logical_or(slot > 0, first == 0)
    keep_even = jnp.logical_or(slot != length, last == 0)
    for parity, (z, keep) in enumerate([(odd_rows, keep_odd), (even_rows, keep_even)]):
        even = shifted(z[0], 1, cols, after_first) + (z[1] + z[2])
        odd = (z[0] + z[1]) + shifted(z[2], -1, cols, before_last)
        pair = []
        for v in (even, odd):
            h = v * 0.5 + half_bias
            h = h + h * jnp.tanh(h)
            pair.append(jnp.where(keep, h, 0.0))
        even, odd = pair
        four = [shifted(odd, 1, cols, after_first), even, odd, shifted(even, -1, cols, before_last)]
        for variant, v in enumerate(four):
            hid[k, variant, :, parity] = v.astype(BF16).reshape(cap + 1, cols, ch)


def gather_taps(hid, f, w2, dims):
    cap, cols, ch = dims
    total = None
    for a in range(3):
        for p in range(3):
            for q in range(3):
                rows = hid[f + a, q : q + 2].reshape(2, 2 * cap + 2, cols, ch)[:, p : p + 2 * cap]
                part = jnp.dot(rows.reshape(4 * cap * cols, ch), w2[a, p, q], preferred_element_type=F32)
                total = part if total is None else total + part
    return total


def finish(total, ext, f, stage, slot, bias, length, frames, dims):
    cap, cols, ch = dims
    total = (total + bias).reshape(2, 2 * cap, cols, ch)
    residual = ext[frames + f, cols : (cap + 1) * cols].astype(F32).reshape(cap, 1, cols, ch)
    residual = jnp.broadcast_to(residual, (cap, 2, cols, ch)).reshape(2 * cap, cols, ch)
    row = lax.broadcasted_iota(jnp.int32, (2 * cap, cols, ch), 0)
    pair = [jnp.where(row < 2 * length, total[c] + residual, 0.0) for c in range(2)]
    stage[slot] = jnp.stack(pair, axis=2).reshape(2 * cap, 2 * cols, ch).astype(BF16)


def extend(raw, ext, k, length, dims):
    cap, cols, ch = dims
    below = raw[k, cap + 1]
    for j in range(cap + 2):
        value = raw[k, j]
        if 2 <= j <= cap:
            value = jnp.where(length + 1 == j, below, value)
        ext[k, j * cols : (j + 1) * cols] = value


def block_kernel(counts, comm, tile_rows, lat, w1_hbm, b1, w2_hbm, b2, out, raw, ext, hid, w1, w2, rim, stage,
                 load_sem, out_sem, rim_send, rim_recv, main_send, main_recv):
    n_tm, n_tile = counts
    frames, cap, cols, ch = lat.shape
    dims = (cap, cols, ch)
    group = lax.axis_index("tm") if comm else jnp.int32(0)
    tile = lax.axis_index("tile") if comm else jnp.int32(5)
    length = tile_rows[tile]
    first, last = (tile == 0).astype(jnp.int32), (tile == n_tile - 1).astype(jnp.int32)
    has_up, has_down = tile > 0, tile < n_tile - 1
    has_next, has_prev = group < n_tm - 1, group > 0

    own = pltpu.make_async_copy(lat, raw.at[frames : 2 * frames, 1 : cap + 1], load_sem.at[0])
    own.start()
    load_one = pltpu.make_async_copy(w1_hbm, w1, load_sem.at[1])
    load_one.start()
    load_two = pltpu.make_async_copy(w2_hbm, w2, load_sem.at[2])
    load_two.start()

    sides = [(0, -1), (0, 1)]
    onward = [(1, 0), (1, -1), (1, 1)]

    def exists(dg, dt):
        ok = jnp.bool_(True)
        if dg > 0:
            ok = jnp.logical_and(ok, has_next)
        if dg < 0:
            ok = jnp.logical_and(ok, has_prev)
        if dt > 0:
            ok = jnp.logical_and(ok, has_down)
        if dt < 0:
            ok = jnp.logical_and(ok, has_up)
        return ok

    def device(dg, dt):
        return (group + dg, tile + dt)

    own.wait()
    for f in range(frames):
        rim[f] = raw[frames + f, length]

    def side_copy(i):
        dt = sides[i][1]
        source = raw.at[frames : 2 * frames, 1] if dt < 0 else rim
        place = cap + 1 if dt < 0 else 0
        return pltpu.make_async_remote_copy(
            src_ref=source, dst_ref=raw.at[frames : 2 * frames, place],
            send_sem=rim_send.at[i], recv_sem=rim_recv.at[i],
            device_id=device(*sides[i]), device_id_type=MESH)

    def onward_copy(i, f):
        dt = onward[i][1]
        if dt == 0:
            source, target = raw.at[frames + f, 1 : cap + 1], raw.at[f, 1 : cap + 1]
        elif dt < 0:
            source, target = raw.at[frames + f, 1], raw.at[f, cap + 1]
        else:
            source, target = rim.at[f], raw.at[f, 0]
        return pltpu.make_async_remote_copy(
            src_ref=source, dst_ref=target,
            send_sem=main_send.at[i, f], recv_sem=main_recv.at[i, f],
            device_id=device(*onward[i]), device_id_type=MESH)

    if comm:
        barrier = pltpu.get_barrier_semaphore()
        for dg, dt in sides + onward:
            @pl.when(exists(-dg, -dt))
            def _():
                pl.semaphore_signal(barrier, inc=1, device_id=device(-dg, -dt), device_id_type=MESH)
        peers = sum(exists(dg, dt).astype(jnp.int32) for dg, dt in sides + onward)
        pl.semaphore_wait(barrier, peers)
        for i in range(2):
            @pl.when(exists(*sides[i]))
            def _():
                side_copy(i).start()
        for f in reversed(range(frames)):
            for i in range(3):
                @pl.when(exists(*onward[i]))
                def _():
                    onward_copy(i, f).start()

    @pl.when(jnp.logical_not(has_up))
    def _():
        for k in range(2 * frames):
            raw[k, 0] = jnp.zeros((cols, ch), BF16)

    @pl.when(jnp.logical_not(has_down))
    def _():
        for k in range(2 * frames):
            raw[k, cap + 1] = jnp.zeros((cols, ch), BF16)

    if comm:
        for i in range(2):
            @pl.when(exists(0, -sides[i][1]))
            def _():
                side_copy(i).wait_recv()
    for k in range(frames, 2 * frames):
        extend(raw, ext, k, length, dims)

    half_bias = b1[...] * 0.5
    args = (w1, half_bias, first, last, length, dims)
    load_one.wait()
    spread(ext, hid, frames + 1, *args)
    spread(ext, hid, frames, *args)
    load_two.wait()
    for f in reversed(range(frames)):
        if comm:
            for i in range(3):
                @pl.when(exists(-onward[i][0], -onward[i][1]))
                def _():
                    onward_copy(i, f).wait_recv()

        @pl.when(has_prev)
        def _():
            extend(raw, ext, f, length, dims)

        @pl.when(jnp.logical_not(has_prev))
        def _():
            ext[f] = ext[frames]

        spread(ext, hid, f, *args)
        total = gather_taps(hid, f, w2, dims)
        finish(total, ext, f, stage, f, b2[...], length, frames, dims)
        pltpu.make_async_copy(stage.at[f], out.at[f], out_sem.at[f]).start()

    if comm:
        for i in range(2):
            @pl.when(exists(*sides[i]))
            def _():
                side_copy(i).wait_send()
        for f in range(frames):
            for i in range(3):
                @pl.when(exists(*onward[i]))
                def _():
                    onward_copy(i, f).wait_send()
    for f in range(frames):
        pltpu.make_async_copy(stage.at[f], out.at[f], out_sem.at[f]).wait()


def run_block(counts, comm, latent, tile_rows, kernel_one, bias_one, kernel_two, bias_two):
    frames, cap, cols, ch = latent.shape
    any_space = pl.BlockSpec(memory_space=pl.ANY)
    vmem = pl.BlockSpec(memory_space=pltpu.VMEM)
    return pl.pallas_call(
        functools.partial(block_kernel, counts, comm),
        out_shape=jax.ShapeDtypeStruct((frames, 2 * cap, 2 * cols, ch), BF16),
        in_specs=[pl.BlockSpec(memory_space=pltpu.SMEM), any_space, any_space, vmem, any_space, vmem],
        out_specs=any_space,
        scratch_shapes=[
            pltpu.VMEM((2 * frames, cap + 2, cols, ch), BF16),
            pltpu.VMEM((2 * frames, (cap + 2) * cols, ch), BF16),
            pltpu.VMEM((frames + 2, 4, cap + 1, 2, cols, ch), BF16),
            pltpu.VMEM(kernel_one.shape, BF16),
            pltpu.VMEM(kernel_two.shape, BF16),
            pltpu.VMEM((frames, cols, ch), BF16),
            pltpu.VMEM((frames, 2 * cap, 2 * cols, ch), BF16),
            pltpu.SemaphoreType.DMA((3,)),
            pltpu.SemaphoreType.DMA((frames,)),
            pltpu.SemaphoreType.DMA((2,)),
            pltpu.SemaphoreType.DMA((2,)),
            pltpu.SemaphoreType.DMA((3, frames)),
            pltpu.SemaphoreType.DMA((3, frames)),
        ],
        compiler_params=pltpu.CompilerParams(
            collective_id=0 if comm else None, has_side_effects=True, vmem_limit_bytes=56 * 2**20),
    )(tile_rows, latent, kernel_one, bias_one.reshape(1, ch), kernel_two, bias_two.reshape(1, ch))


def solution(mesh):
    counts = (mesh.shape["tm"], mesh.shape["tile"])
    in_specs = (P("tm", "tile", None, None), P(), P(), P(), P(), P())
    return jax.shard_map(functools.partial(run_block, counts, True), mesh=mesh, in_specs=in_specs,
                         out_specs=P("tm", "tile", None, None), check_vma=False)
```

```python
import functools

import jax
import jax.numpy as jnp
from jax import lax
from jax.experimental import pallas as pl
from jax.experimental.pallas import tpu as pltpu
from jax.sharding import PartitionSpec as P

MESH = pl.DeviceIdType.MESH
F32, BF16 = jnp.float32, jnp.bfloat16


def shifted(value, by, cols):
    edge = lax.broadcasted_iota(jnp.int32, (8, value.shape[1]), 0)
    moved = pltpu.roll(value, by % value.shape[0], axis=0)
    pieces = []
    for start in range(0, value.shape[0], cols):
        if by > 0:
            pieces += [jnp.where(edge != 0, moved[start : start + 8], 0.0), moved[start + 8 : start + cols]]
        else:
            pieces += [moved[start : start + cols - 8],
                       jnp.where(edge != 7, moved[start + cols - 8 : start + cols], 0.0)]
    return jnp.concatenate(pieces, axis=0)


class Frames:
    def __init__(self, ref):
        self.ref = ref

    def __getitem__(self, k):
        return self.ref.at[k]


def spread(ext, hid, k, w1, half_bias, first, last, length, dims):
    cap, cols, ch = dims
    n = (cap + 1) * cols
    taps = jnp.concatenate([ext[k], ext[k + 1], ext[k + 2]], axis=1)
    upper, lower = taps[:n], taps[cols:]
    ends = jnp.concatenate([upper, lower], axis=1)
    even_rows, odd_rows = [], []
    for q in range(3):
        outer = jnp.concatenate([w1[:, 0, q].reshape(3 * ch, ch), w1[:, 2, q].reshape(3 * ch, ch)], axis=0)
        shared = jnp.dot(ends, outer, preferred_element_type=F32)
        centre = jnp.dot(taps, w1[:, 1, q].reshape(3 * ch, ch), preferred_element_type=F32)
        even_rows.append(shared + centre[cols:])
        odd_rows.append(shared + centre[:n])
    outside_odd = [first == 1] + [None] * cap
    outside_even = [jnp.logical_and(last == 1, length == j) if j else None for j in range(cap + 1)]
    for parity, (z, outside) in enumerate([(odd_rows, outside_odd), (even_rows, outside_even)]):
        even = shifted(z[0], 1, cols) + (z[1] + z[2])
        odd = (z[0] + z[1]) + shifted(z[2], -1, cols)
        pair = []
        for v in (even, odd):
            h = v * 0.5 + half_bias
            h = h + h * jnp.tanh(h)
            slots = [h[j * cols : (j + 1) * cols] for j in range(cap + 1)]
            slots = [x if o is None else jnp.where(o, 0.0, x) for x, o in zip(slots, outside)]
            pair.append(jnp.concatenate(slots, axis=0))
        even, odd = pair
        four = [shifted(odd, 1, cols), even, odd, shifted(even, -1, cols)]
        for variant, v in enumerate(four):
            hid[k][variant, :, parity] = v.astype(BF16).reshape(cap + 1, cols, ch)


def gather_taps(hid, f, w2, dims, taps=(2, 1, 0), rest=None):
    cap, cols, ch = dims
    total = None
    for a in taps:
        for p in range(3):
            for q in range(3):
                rows = hid[f + a][q : q + 2].reshape(2, 2 * cap + 2, cols, ch)[:, p : p + 2 * cap]
                part = jnp.dot(rows.reshape(4 * cap * cols, ch), w2[a, p, q], preferred_element_type=F32)
                total = part if total is None else total + part
    return total if rest is None else total + rest


def finish(total, ext, f, woven, stage, slot, bias, length, frames, dims):
    cap, cols, ch = dims
    total = total.reshape(2, 2 * cap, cols, ch)
    half = ch // 2
    for r in range(cap):
        residual = ext[frames + f, (r + 1) * cols : (r + 2) * cols].astype(F32) + bias
        for y in range(2 * r, 2 * r + 2):
            for c in range(2):
                value = total[c, y] + residual
                if r > 0:
                    value = jnp.where(r < length, value, 0.0)
                for h in range(2):
                    woven[slot, h, pl.ds(2 * cols * y + c, cols, stride=2)] = value[:, h * half : (h + 1) * half]
    for h in range(2):
        stage[slot, :, :, h * half : (h + 1) * half] = woven[slot, h].astype(BF16).reshape(2 * cap, 2 * cols, half)


def extend(rims, rows, ext, k, late, edges, dims):
    cap, cols, ch = dims
    has_up, has_down, has_prev, length, frames = edges
    above, below = (jnp.where(there, rims[i, k], jnp.zeros((cols, ch), BF16)) for i, there in enumerate((has_up, has_down)))
    for j in range(cap + 2):
        value = above if j == 0 else below if j == cap + 1 else rows[j - 1]
        if 2 <= j <= cap:
            value = jnp.where(length + 1 == j, below, value)
        place = slice(j * cols, (j + 1) * cols)
        if late:
            value = jnp.where(has_prev, value, ext[frames, place])
        ext[k, place] = value


def block_kernel(counts, comm, tile_rows, lat, w1_hbm, b1, w2_hbm, b2, out, mine, rims, halo, ext, hidden, w1, w2, rim, stage, woven,
                 load_sem, out_sem, side_send, side_recv, next_send, next_recv):
    n_tm, n_tile = counts
    frames, cap, cols, ch = lat.shape
    dims = (cap, cols, ch)
    group = lax.axis_index("tm") if comm else tile_rows[0] + 1
    tile = lax.axis_index("tile") if comm else tile_rows[1] + 3
    length = tile_rows[tile]
    first, last = (tile == 0).astype(jnp.int32), (tile == n_tile - 1).astype(jnp.int32)
    has_up, has_down, has_next, has_prev = tile > 0, tile < n_tile - 1, group < n_tm - 1, group > 0
    edges = (has_up, has_down, has_prev, length, frames)

    own = pltpu.make_async_copy(lat, mine, load_sem.at[0])
    own.start()
    load_one = pltpu.make_async_copy(w1_hbm, w1, load_sem.at[1])
    load_one.start()
    load_two = pltpu.make_async_copy(w2_hbm, w2, load_sem.at[2])
    load_two.start()

    sides = [(0, -1), (0, 1)]
    onward = [(1, 0), (1, -1), (1, 1)]

    def exists(dg, dt):
        ok = jnp.bool_(True)
        for step, there in ((dg, has_next if dg > 0 else has_prev), (dt, has_down if dt > 0 else has_up)):
            ok = jnp.logical_and(ok, there) if step else ok
        return ok

    def remote(source, target, send, recv, dg, dt):
        return pltpu.make_async_remote_copy(src_ref=source, dst_ref=target, send_sem=send, recv_sem=recv,
                                            device_id=(group + dg, tile + dt), device_id_type=MESH)

    def side_copy(i):
        source = (mine.at[:, 0], rim)[i]
        return remote(source, rims.at[1 - i, frames : 2 * frames], side_send.at[i], side_recv.at[i], *sides[i])

    def onward_copy(i, f):
        source, target = ((mine.at[f], halo.at[f]), (mine.at[f, 0], rims.at[1, f]), (rim.at[f], rims.at[0, f]))[i]
        return remote(source, target, next_send.at[i, f], next_recv.at[i, f], *onward[i])

    def lay(k):
        extend(rims, mine.at[k - frames], ext, k, False, edges, dims)

    def arrive(*late):
        for f in late:
            if comm:
                for i, (dg, dt) in enumerate(onward):
                    @pl.when(exists(-dg, -dt))
                    def _():
                        onward_copy(i, f).wait_recv()
            else:
                @pl.when(has_prev)
                def _():
                    pltpu.make_async_copy(lat.at[f], halo.at[f], next_recv.at[0, f]).wait()
        for f in late:
            extend(rims, halo.at[f], ext, f, True, edges, dims)

    if comm:
        barrier = pltpu.get_barrier_semaphore()
        for dg, dt in sides + onward:
            @pl.when(exists(-dg, -dt))
            def _():
                pl.semaphore_signal(barrier, inc=1, device_id=(group - dg, tile - dt), device_id_type=MESH)
    else:
        for f in range(frames):
            pltpu.make_async_copy(lat.at[f], halo.at[f], next_recv.at[0, f]).start()
    own.wait()
    for f in range(frames):
        rim[f] = mine[f, jnp.maximum(length - 1, 0)]
    if comm:
        pl.semaphore_wait(barrier, sum(exists(dg, dt).astype(jnp.int32) for dg, dt in sides + onward))
        for i in range(2):
            @pl.when(exists(*sides[i]))
            def _():
                side_copy(i).start()
        for f in reversed(range(frames)):
            for i in range(3):
                @pl.when(exists(*onward[i]))
                def _():
                    onward_copy(i, f).start()
        for i, (dg, dt) in enumerate(sides):
            @pl.when(exists(-dg, -dt))
            def _():
                side_copy(i).wait_recv()

    for k in range(frames, 2 * frames):
        lay(k)
    hid = Frames(hidden)
    args = (w1, b1[...] * 0.5, first, last, length, dims)

    def out_copy(f):
        return pltpu.make_async_copy(stage.at[f], out.at[f], out_sem.at[f])

    def last_step(total, f):
        finish(total, ext, f, woven, stage, f, b2[...], length, frames, dims)
        out_copy(f).start()

    load_one.wait()
    load_two.wait()
    spread(ext, hid, 5, *args)
    spread(ext, hid, 4, *args)

    def step(i, carry):
        f = frames - 1 - i
        arrive(f)
        spread(ext, hid, f, *args)
        last_step(gather_taps(hid, f, w2, dims), f)
        return carry

    lax.fori_loop(0, frames, step, 0)

    if comm:
        for i in range(2):
            @pl.when(exists(*sides[i]))
            def _():
                side_copy(i).wait_send()
        for f in range(frames):
            for i in range(3):
                @pl.when(exists(*onward[i]))
                def _():
                    onward_copy(i, f).wait_send()
    for f in range(frames):
        out_copy(f).wait()


def run_block(counts, comm, latent, tile_rows, kernel_one, bias_one, kernel_two, bias_two):
    frames, cap, cols, ch = latent.shape
    in_hbm = pl.BlockSpec(memory_space=pl.ANY)
    vmem = pl.BlockSpec(memory_space=pltpu.VMEM)
    smem = pl.BlockSpec(memory_space=pltpu.SMEM)
    dma = pltpu.SemaphoreType.DMA
    return pl.pallas_call(
        functools.partial(block_kernel, counts, comm),
        out_shape=jax.ShapeDtypeStruct((frames, 2 * cap, 2 * cols, ch), BF16),
        in_specs=[smem, in_hbm, in_hbm, vmem, in_hbm, vmem],
        out_specs=in_hbm,
        scratch_shapes=[
            pltpu.VMEM((frames, cap, cols, ch), BF16),
            pltpu.VMEM((2, 2 * frames, cols, ch), BF16),
            pltpu.VMEM((frames, cap, cols, ch), BF16),
            pltpu.VMEM((2 * frames, (cap + 2) * cols, ch), BF16),
            pltpu.VMEM((frames + 2, 4, cap + 1, 2, cols, ch), BF16),
            pltpu.VMEM(kernel_one.shape, BF16),
            pltpu.VMEM(kernel_two.shape, BF16),
            pltpu.VMEM((frames, cols, ch), BF16),
            pltpu.VMEM((frames, 2 * cap, 2 * cols, ch), BF16),
            pltpu.VMEM((frames, 2, 4 * cap * cols, ch // 2), F32),
            dma((3,)), dma((frames,)), dma((2,)), dma((2,)), dma((3, frames)), dma((3, frames)),
        ],
        compiler_params=pltpu.CompilerParams(
            collective_id=0 if comm else None, has_side_effects=True, vmem_limit_bytes=56 * 2**20),
    )(tile_rows, latent, kernel_one, bias_one.reshape(1, ch), kernel_two, bias_two.reshape(1, ch))


def solution(mesh):
    counts = (mesh.shape["tm"], mesh.shape["tile"])
    in_specs = (P("tm", "tile", None, None), P(), P(), P(), P(), P())
    return jax.shard_map(functools.partial(run_block, counts, True), mesh=mesh, in_specs=in_specs,
                         out_specs=P("tm", "tile", None, None), check_vma=False)
```

```python
import functools

import jax
import jax.numpy as jnp
from jax import lax
from jax.experimental import pallas as pl
from jax.experimental.pallas import tpu as pltpu
from jax.sharding import PartitionSpec as P

MESH = pl.DeviceIdType.MESH
F32, BF16 = jnp.float32, jnp.bfloat16


def shifted(value, by, cols):
    edge = lax.broadcasted_iota(jnp.int32, (8, value.shape[1]), 0)
    moved = pltpu.roll(value, by % value.shape[0], axis=0)
    pieces = []
    for start in range(0, value.shape[0], cols):
        if by > 0:
            pieces += [jnp.where(edge != 0, moved[start : start + 8], 0.0), moved[start + 8 : start + cols]]
        else:
            pieces += [moved[start : start + cols - 8],
                       jnp.where(edge != 7, moved[start + cols - 8 : start + cols], 0.0)]
    return jnp.concatenate(pieces, axis=0)


class Frames:
    def __init__(self, ref, base):
        self.ref, self.base = ref, base

    def __getitem__(self, k):
        return self.ref.at[k - self.base]


def spread(ext, hid, k, w1, half_bias, first, last, length, dims):
    cap, cols, ch = dims
    n = (cap + 1) * cols
    taps = jnp.concatenate([ext[k], ext[k + 1], ext[k + 2]], axis=1)
    upper, lower = taps[:n], taps[cols:]
    ends = jnp.concatenate([upper, lower], axis=1)
    even_rows, odd_rows = [], []
    for q in range(3):
        outer = jnp.concatenate([w1[:, 0, q].reshape(3 * ch, ch), w1[:, 2, q].reshape(3 * ch, ch)], axis=0)
        shared = jnp.dot(ends, outer, preferred_element_type=F32)
        centre = jnp.dot(taps, w1[:, 1, q].reshape(3 * ch, ch), preferred_element_type=F32)
        even_rows.append(shared + centre[cols:])
        odd_rows.append(shared + centre[:n])
    outside_odd = [first == 1] + [None] * cap
    outside_even = [jnp.logical_and(last == 1, length == j) if j else None for j in range(cap + 1)]
    for parity, (z, outside) in enumerate([(odd_rows, outside_odd), (even_rows, outside_even)]):
        even = shifted(z[0], 1, cols) + (z[1] + z[2])
        odd = (z[0] + z[1]) + shifted(z[2], -1, cols)
        pair = []
        for v in (even, odd):
            h = v * 0.5 + half_bias
            h = h + h * jnp.tanh(h)
            slots = [h[j * cols : (j + 1) * cols] for j in range(cap + 1)]
            slots = [x if o is None else jnp.where(o, 0.0, x) for x, o in zip(slots, outside)]
            pair.append(jnp.concatenate(slots, axis=0))
        even, odd = pair
        four = [shifted(odd, 1, cols), even, odd, shifted(even, -1, cols)]
        for variant, v in enumerate(four):
            hid[k][variant, :, parity] = v.astype(BF16).reshape(cap + 1, cols, ch)


def gather_taps(hid, f, w2, dims, taps=(2, 1, 0), rest=None):
    cap, cols, ch = dims
    total = None
    for a in taps:
        for p in range(3):
            for q in range(3):
                rows = hid[f + a][q : q + 2].reshape(2, 2 * cap + 2, cols, ch)[:, p : p + 2 * cap]
                part = jnp.dot(rows.reshape(4 * cap * cols, ch), w2[a, p, q], preferred_element_type=F32)
                total = part if total is None else total + part
    return total if rest is None else total + rest


def finish(total, ext, f, woven, stage, slot, bias, length, frames, dims):
    cap, cols, ch = dims
    total = total.reshape(2, 2 * cap, cols, ch)
    half = ch // 2
    for r in range(cap):
        residual = ext[frames + f, (r + 1) * cols : (r + 2) * cols].astype(F32) + bias
        for y in range(2 * r, 2 * r + 2):
            for c in range(2):
                value = total[c, y] + residual
                if r > 0:
                    value = jnp.where(r < length, value, 0.0)
                for h in range(2):
                    woven[slot, h, pl.ds(2 * cols * y + c, cols, stride=2)] = value[:, h * half : (h + 1) * half]
    for h in range(2):
        stage[slot, :, :, h * half : (h + 1) * half] = woven[slot, h].astype(BF16).reshape(2 * cap, 2 * cols, half)


def extend(rims, rows, ext, k, late, edges, dims):
    cap, cols, ch = dims
    has_up, has_down, has_prev, length, frames = edges
    above, below = (jnp.where(there, rims[i, k], jnp.zeros((cols, ch), BF16)) for i, there in enumerate((has_up, has_down)))
    for j in range(cap + 2):
        value = above if j == 0 else below if j == cap + 1 else rows[j - 1]
        if 2 <= j <= cap:
            value = jnp.where(length + 1 == j, below, value)
        place = slice(j * cols, (j + 1) * cols)
        if late:
            value = jnp.where(has_prev, value, ext[frames, place])
        ext[k, place] = value


def place_of(comm, counts, tile_rows):
    group = lax.axis_index("tm") if comm else tile_rows[0] + 1
    tile = lax.axis_index("tile") if comm else tile_rows[1] + 3
    return group, tile, tile_rows[tile], (tile == 0).astype(jnp.int32), (tile == counts[1] - 1).astype(jnp.int32)


def early_kernel(counts, comm, tile_rows, lat, w1_hbm, b1, w2_hbm, b2, hid_late, ext, w1, w2, stage, partial, mine, rims, halo, rim, woven,
                 load_sem, side_send, side_recv, next_send, next_recv):
    n_tm, n_tile = counts
    frames, cap, cols, ch = lat.shape
    dims = (cap, cols, ch)
    group, tile, length, first, last = place_of(comm, counts, tile_rows)
    has_up, has_down, has_next, has_prev = tile > 0, tile < n_tile - 1, group < n_tm - 1, group > 0
    edges = (has_up, has_down, has_prev, length, frames)

    own = pltpu.make_async_copy(lat, mine, load_sem.at[0])
    own.start()
    load_one = pltpu.make_async_copy(w1_hbm, w1, load_sem.at[1])
    load_one.start()
    load_two = pltpu.make_async_copy(w2_hbm, w2, load_sem.at[2])
    load_two.start()

    sides = [(0, -1), (0, 1)]
    onward = [(1, 0), (1, -1), (1, 1)]

    def exists(dg, dt):
        ok = jnp.bool_(True)
        for step, there in ((dg, has_next if dg > 0 else has_prev), (dt, has_down if dt > 0 else has_up)):
            ok = jnp.logical_and(ok, there) if step else ok
        return ok

    def remote(source, target, send, recv, dg, dt):
        return pltpu.make_async_remote_copy(src_ref=source, dst_ref=target, send_sem=send, recv_sem=recv,
                                            device_id=(group + dg, tile + dt), device_id_type=MESH)

    def side_copy(i):
        source = (mine.at[:, 0], rim)[i]
        return remote(source, rims.at[1 - i, frames : 2 * frames], side_send.at[i], side_recv.at[i], *sides[i])

    def onward_copy(i, f):
        source, target = ((mine.at[f], halo.at[f]), (mine.at[f, 0], rims.at[1, f]), (rim.at[f], rims.at[0, f]))[i]
        return remote(source, target, next_send.at[i, f], next_recv.at[i, f], *onward[i])

    def lay(k):
        extend(rims, mine.at[k - frames], ext, k, False, edges, dims)

    def arrive(*late):
        for f in late:
            if comm:
                for i, (dg, dt) in enumerate(onward):
                    @pl.when(exists(-dg, -dt))
                    def _():
                        onward_copy(i, f).wait_recv()
            else:
                @pl.when(has_prev)
                def _():
                    pltpu.make_async_copy(lat.at[f], halo.at[f], next_recv.at[0, f]).wait()
        for f in late:
            extend(rims, halo.at[f], ext, f, True, edges, dims)

    if comm:
        barrier = pltpu.get_barrier_semaphore()
        for dg, dt in sides + onward:
            @pl.when(exists(-dg, -dt))
            def _():
                pl.semaphore_signal(barrier, inc=1, device_id=(group - dg, tile - dt), device_id_type=MESH)
    else:
        for f in range(frames):
            pltpu.make_async_copy(lat.at[f], halo.at[f], next_recv.at[0, f]).start()
    own.wait()
    for f in range(frames):
        rim[f] = mine[f, jnp.maximum(length - 1, 0)]
    if comm:
        pl.semaphore_wait(barrier, sum(exists(dg, dt).astype(jnp.int32) for dg, dt in sides + onward))
        for i in range(2):
            @pl.when(exists(*sides[i]))
            def _():
                side_copy(i).start()
        for f in reversed(range(frames)):
            for i in range(3):
                @pl.when(exists(*onward[i]))
                def _():
                    onward_copy(i, f).start()
        for i, (dg, dt) in enumerate(sides):
            @pl.when(exists(-dg, -dt))
            def _():
                side_copy(i).wait_recv()

    for k in range(frames, 2 * frames):
        lay(k)
    half = frames // 2
    hid = Frames(hid_late, half)
    args = (w1, b1[...] * 0.5, first, last, length, dims)
    load_one.wait()
    load_two.wait()
    spread(ext, hid, 5, *args)
    spread(ext, hid, 4, *args)
    partial[...] = gather_taps(hid, frames - 1, w2, dims, (2, 1))

    def step(i, carry):
        f = frames - 1 - i
        arrive(f)
        spread(ext, hid, f, *args)
        total = gather_taps(hid, f, w2, dims, (0,), partial[...])
        coming = gather_taps(hid, f - 1, w2, dims, (2, 1))
        finish(total, ext, f, woven, stage, f - half, b2[...], length, frames, dims)
        partial[...] = coming
        return carry

    lax.fori_loop(0, half, step, 0)
    arrive(*reversed(range(half)))

    if comm:
        for i in range(2):
            @pl.when(exists(*sides[i]))
            def _():
                side_copy(i).wait_send()
        for f in range(frames):
            for i in range(3):
                @pl.when(exists(*onward[i]))
                def _():
                    onward_copy(i, f).wait_send()


def late_kernel(counts, comm, tile_rows, hid_late, ext, w1, w2, stage_late, partial, b1, b2, out, hid_early, stage, woven, out_sem):
    frames, cap, cols, ch = out.shape[0], out.shape[1] // 2, out.shape[2] // 2, out.shape[3]
    dims = (cap, cols, ch)
    half = frames // 2
    _, _, length, first, last = place_of(comm, counts, tile_rows)
    early, late = Frames(hid_early, 0), Frames(hid_late, half)
    hid = [early[k] if k < half else late[k] for k in range(frames + 2)]
    args = (w1, b1[...] * 0.5, first, last, length, dims)

    def out_copy(f):
        source = stage.at[f] if f < half else stage_late.at[f - half]
        return pltpu.make_async_copy(source, out.at[f], out_sem.at[f])

    for f in range(half, frames):
        out_copy(f).start()
    for f in reversed(range(half)):
        spread(ext, hid, f, *args)
    for f in reversed(range(half)):
        taps = (0,) if f == half - 1 else (2, 1, 0)
        total = gather_taps(hid, f, w2, dims, taps, partial[...] if f == half - 1 else None)
        finish(total, ext, f, woven, stage, f, b2[...], length, frames, dims)
        out_copy(f).start()
    for f in range(frames):
        out_copy(f).wait()


def run_block(counts, comm, latent, tile_rows, kernel_one, bias_one, kernel_two, bias_two):
    frames, cap, cols, ch = latent.shape
    half = frames // 2
    in_hbm = pl.BlockSpec(memory_space=pl.ANY)
    vmem = pl.BlockSpec(memory_space=pltpu.VMEM)
    smem = pl.BlockSpec(memory_space=pltpu.SMEM)
    dma = pltpu.SemaphoreType.DMA
    hidden = (4, cap + 1, 2, cols, ch)
    frame = (2 * cap, 2 * cols, ch)
    woven = (half, 2, 4 * cap * cols, ch // 2)
    bias_one, bias_two = bias_one.reshape(1, ch), bias_two.reshape(1, ch)
    kept = pl.pallas_call(
        functools.partial(early_kernel, counts, comm),
        out_shape=(
            pltpu.VMEM((frames + 2 - half, *hidden), BF16),
            pltpu.VMEM((2 * frames, (cap + 2) * cols, ch), BF16),
            pltpu.VMEM(kernel_one.shape, BF16),
            pltpu.VMEM(kernel_two.shape, BF16),
            pltpu.VMEM((half, *frame), BF16),
            pltpu.VMEM((4 * cap * cols, ch), F32),
        ),
        in_specs=[smem, in_hbm, in_hbm, vmem, in_hbm, vmem],
        out_specs=[vmem] * 6,
        scratch_shapes=[
            pltpu.VMEM((frames, cap, cols, ch), BF16),
            pltpu.VMEM((2, 2 * frames, cols, ch), BF16),
            pltpu.VMEM((frames, cap, cols, ch), BF16),
            pltpu.VMEM((frames, cols, ch), BF16),
            pltpu.VMEM(woven, F32),
            dma((3,)), dma((2,)), dma((2,)), dma((3, frames)), dma((3, frames)),
        ],
        compiler_params=pltpu.CompilerParams(
            collective_id=0 if comm else None, has_side_effects=True, vmem_limit_bytes=44 * 2**20),
    )(tile_rows, latent, kernel_one, bias_one, kernel_two, bias_two)
    return pl.pallas_call(
        functools.partial(late_kernel, counts, comm),
        out_shape=jax.ShapeDtypeStruct((frames, *frame), BF16),
        in_specs=[smem] + [vmem] * 8,
        out_specs=in_hbm,
        scratch_shapes=[
            pltpu.VMEM((half, *hidden), BF16),
            pltpu.VMEM((half, *frame), BF16),
            pltpu.VMEM(woven, F32),
            dma((frames,)),
        ],
        compiler_params=pltpu.CompilerParams(vmem_limit_bytes=40 * 2**20),
    )(tile_rows, *kept, bias_one, bias_two)


def solution(mesh):
    counts = (mesh.shape["tm"], mesh.shape["tile"])
    in_specs = (P("tm", "tile", None, None), P(), P(), P(), P(), P())
    return jax.shard_map(functools.partial(run_block, counts, True), mesh=mesh, in_specs=in_specs,
                         out_specs=P("tm", "tile", None, None), check_vma=False)
```

```python
import functools

import jax
import jax.numpy as jnp
from jax import lax
from jax.experimental import pallas as pl
from jax.experimental.pallas import tpu as pltpu
from jax.sharding import PartitionSpec as P

MESH = pl.DeviceIdType.MESH
F32, BF16 = jnp.float32, jnp.bfloat16


def shifted(value, by, cols):
    edge = lax.broadcasted_iota(jnp.int32, (8, value.shape[1]), 0)
    moved = pltpu.roll(value, by % value.shape[0], axis=0)
    pieces = []
    for start in range(0, value.shape[0], cols):
        if by > 0:
            pieces += [jnp.where(edge != 0, moved[start : start + 8], 0.0), moved[start + 8 : start + cols]]
        else:
            pieces += [moved[start : start + cols - 8],
                       jnp.where(edge != 7, moved[start + cols - 8 : start + cols], 0.0)]
    return jnp.concatenate(pieces, axis=0)


class Frames:
    def __init__(self, ref, base):
        self.ref, self.base = ref, base

    def __getitem__(self, k):
        return self.ref.at[k - self.base]


def tap_products(taps, w1, dims, above=True):
    cap, cols, ch = dims
    n = (cap + 1) * cols
    ends = jnp.concatenate([taps[:n], taps[cols:]], axis=1)
    even_rows, odd_rows = [], []
    for q in range(3):
        outer = jnp.concatenate([w1[:, 0, q].reshape(3 * ch, ch), w1[:, 2, q].reshape(3 * ch, ch)], axis=0)
        shared = jnp.dot(ends, outer, preferred_element_type=F32)
        centre = jnp.dot(taps, w1[:, 1, q].reshape(3 * ch, ch), preferred_element_type=F32)
        even_rows.append(shared + centre[cols:])
        odd = shared + centre[:n] if above else jnp.concatenate([shared[:cols], shared[cols:] + centre[cols:n]], axis=0)
        odd_rows.append(odd)
    return even_rows, odd_rows


def activate(even_rows, odd_rows, hid, k, half_bias, first, last, length, dims):
    cap, cols, ch = dims
    outside_odd = [first == 1] + [None] * cap
    outside_even = [jnp.logical_and(last == 1, length == j) if j else None for j in range(cap + 1)]
    for parity, (z, outside) in enumerate([(odd_rows, outside_odd), (even_rows, outside_even)]):
        even = shifted(z[0], 1, cols) + (z[1] + z[2])
        odd = (z[0] + z[1]) + shifted(z[2], -1, cols)
        pair = []
        for v in (even, odd):
            h = v * 0.5 + half_bias
            h = h + h * jnp.tanh(h)
            slots = [h[j * cols : (j + 1) * cols] for j in range(cap + 1)]
            slots = [x if o is None else jnp.where(o, 0.0, x) for x, o in zip(slots, outside)]
            pair.append(jnp.concatenate(slots, axis=0))
        even, odd = pair
        four = [shifted(odd, 1, cols), even, odd, shifted(even, -1, cols)]
        for variant, v in enumerate(four):
            hid[k][variant, :, parity] = v.astype(BF16).reshape(cap + 1, cols, ch)


def frame_taps(ext, k):
    return jnp.concatenate([ext[k], ext[k + 1], ext[k + 2]], axis=1)


def spread(ext, hid, k, w1, half_bias, first, last, length, dims):
    activate(*tap_products(frame_taps(ext, k), w1, dims), hid, k, half_bias, first, last, length, dims)


def add_edges(before, edge, base, ks, hid, w1, half_bias, first, last, length, dims):
    cap, cols, ch = dims
    upper, lower = (
        jnp.concatenate([jnp.concatenate([edge[i, k - base + a] for a in range(3)], axis=1) for k in ks], axis=0)
        for i in range(2))
    terms = []
    for q in range(3):
        weights = [w1[:, p, q].reshape(3 * ch, ch) for p in range(3)]
        pairs = ((upper, 0), (upper, 1), (lower, 1), (lower, 2))
        terms.append([jnp.dot(x, weights[p], preferred_element_type=F32) for x, p in pairs])
    for i, k in enumerate(ks):
        even_rows, odd_rows = [], []
        for q in range(3):
            at = slice(i * cols, (i + 1) * cols)
            above_0, above_1, below_1, below_2 = (term[at] for term in terms[q])
            for rows, own, top, bottom in ((even_rows, before[i, 0, q], above_0, below_1 + below_2),
                                           (odd_rows, before[i, 1, q], above_0 + above_1, below_2)):
                slots = [own[:cols] + top]
                for j in range(1, cap + 1):
                    slots.append(own[j * cols : (j + 1) * cols] + jnp.where(length == j, bottom, 0.0))
                rows.append(jnp.concatenate(slots, axis=0))
        activate(even_rows, odd_rows, hid, k, half_bias, first, last, length, dims)


def gather_taps(hid, f, w2, dims, part, taps=(2, 1, 0), rest=None):
    cap, cols, ch = dims
    total = None
    for a in taps:
        for p in range(3):
            for q in range(3):
                start = p + part * cap
                rows = hid[f + a][q : q + 2].reshape(2, 2 * cap + 2, cols, ch)[:, start : start + cap]
                term = jnp.dot(rows.reshape(2 * cap * cols, ch), w2[a, p, q], preferred_element_type=F32)
                total = term if total is None else total + term
    return total if rest is None else total + rest


def finish(total, ext, f, woven, stage, slot, bias, length, frames, dims, part):
    cap, cols, ch = dims
    total = total.reshape(2, cap, cols, ch)
    half = ch // 2
    for r in range(part * cap // 2, (part + 1) * cap // 2):
        residual = ext[frames + f, (r + 1) * cols : (r + 2) * cols].astype(F32) + bias
        for y in range(2 * r, 2 * r + 2):
            for c in range(2):
                value = total[c, y - part * cap] + residual
                if r > 0:
                    value = jnp.where(r < length, value, 0.0)
                for h in range(2):
                    woven[slot, h, pl.ds(2 * cols * y + c, cols, stride=2)] = value[:, h * half : (h + 1) * half]
    rows, flat = slice(part * cap, (part + 1) * cap), slice(2 * cols * part * cap, 2 * cols * (part + 1) * cap)
    for h in range(2):
        stage[slot, rows, :, h * half : (h + 1) * half] = woven[slot, h, flat].astype(BF16).reshape(cap, 2 * cols, half)


def extend(rims, rows, ext, k, late, edges, dims):
    cap, cols, ch = dims
    has_up, has_down, has_prev, length, frames = edges
    above, below = (jnp.where(there, rims[i, k], jnp.zeros((cols, ch), BF16)) for i, there in enumerate((has_up, has_down)))
    for j in range(cap + 2):
        value = above if j == 0 else below if j == cap + 1 else rows[j - 1]
        if 2 <= j <= cap:
            value = jnp.where(length + 1 == j, below, value)
        place = slice(j * cols, (j + 1) * cols)
        if late:
            value = jnp.where(has_prev, value, ext[frames, place])
        ext[k, place] = value


def place_of(comm, counts, tile_rows):
    group = lax.axis_index("tm") if comm else tile_rows[0] + 1
    tile = lax.axis_index("tile") if comm else tile_rows[1] + 3
    return group, tile, tile_rows[tile], (tile == 0).astype(jnp.int32), (tile == counts[1] - 1).astype(jnp.int32)


def early_kernel(counts, comm, tile_rows, lat, w1_hbm, b1, w2_hbm, b2, hid_late, ext, w1, w2, stage, partial, mine, rims, halo, rim, woven, edge, before,
                 load_sem, side_send, side_recv, next_send, next_recv):
    n_tm, n_tile = counts
    frames, cap, cols, ch = lat.shape
    dims = (cap, cols, ch)
    group, tile, length, first, last = place_of(comm, counts, tile_rows)
    has_up, has_down, has_next, has_prev = tile > 0, tile < n_tile - 1, group < n_tm - 1, group > 0
    edges = (has_up, has_down, has_prev, length, frames)

    own = pltpu.make_async_copy(lat, mine, load_sem.at[0])
    own.start()
    load_one = pltpu.make_async_copy(w1_hbm, w1, load_sem.at[1])
    load_one.start()
    load_two = pltpu.make_async_copy(w2_hbm, w2, load_sem.at[2])
    load_two.start()

    sides = [(0, -1), (0, 1)]
    onward = [(1, 0), (1, -1), (1, 1)]

    def exists(dg, dt):
        ok = jnp.bool_(True)
        for step, there in ((dg, has_next if dg > 0 else has_prev), (dt, has_down if dt > 0 else has_up)):
            ok = jnp.logical_and(ok, there) if step else ok
        return ok

    def remote(source, target, send, recv, dg, dt):
        return pltpu.make_async_remote_copy(src_ref=source, dst_ref=target, send_sem=send, recv_sem=recv,
                                            device_id=(group + dg, tile + dt), device_id_type=MESH)

    def side_copy(i):
        source = (mine.at[:, 0], rim)[i]
        return remote(source, rims.at[1 - i, frames : 2 * frames], side_send.at[i], side_recv.at[i], *sides[i])

    def onward_copy(i, f):
        source, target = ((mine.at[f], halo.at[f]), (mine.at[f, 0], rims.at[1, f]), (rim.at[f], rims.at[0, f]))[i]
        return remote(source, target, next_send.at[i, f], next_recv.at[i, f], *onward[i])

    def lay(k):
        extend(rims, mine.at[k - frames], ext, k, False, edges, dims)

    def arrive(*late):
        for f in late:
            if comm:
                for i, (dg, dt) in enumerate(onward):
                    @pl.when(exists(-dg, -dt))
                    def _():
                        onward_copy(i, f).wait_recv()
            else:
                @pl.when(has_prev)
                def _():
                    pltpu.make_async_copy(lat.at[f], halo.at[f], next_recv.at[0, f]).wait()
        for f in late:
            extend(rims, halo.at[f], ext, f, True, edges, dims)

    if comm:
        barrier = pltpu.get_barrier_semaphore()
        for dg, dt in sides + onward:
            @pl.when(exists(-dg, -dt))
            def _():
                pl.semaphore_signal(barrier, inc=1, device_id=(group - dg, tile - dt), device_id_type=MESH)
    else:
        for f in range(frames):
            pltpu.make_async_copy(lat.at[f], halo.at[f], next_recv.at[0, f]).start()
    own.wait()
    for f in range(frames):
        rim[f] = mine[f, jnp.maximum(length - 1, 0)]
    if comm:
        pl.semaphore_wait(barrier, sum(exists(dg, dt).astype(jnp.int32) for dg, dt in sides + onward))
        for i in range(2):
            @pl.when(exists(*sides[i]))
            def _():
                side_copy(i).start()
        for f in reversed(range(frames)):
            for i in range(3):
                @pl.when(exists(*onward[i]))
                def _():
                    onward_copy(i, f).start()

    half = frames // 2
    hid = Frames(hid_late, half)
    args = (w1, b1[...] * 0.5, first, last, length, dims)

    for k in range(frames):
        for j in range(cap + 2):
            value = jnp.zeros((cols, ch), BF16)
            if 1 <= j <= cap:
                value = mine[k, j - 1] if j == 1 else jnp.where(j <= length, mine[k, j - 1], value)
            ext[frames + k, j * cols : (j + 1) * cols] = value
    load_one.wait()
    alone = (frames + 1, frames)
    for i, k in enumerate(alone):
        for parity, rows in enumerate(tap_products(frame_taps(ext, k), w1, dims, False)):
            for q in range(3):
                before[i, parity, q] = rows[q]
    if comm:
        for i, (dg, dt) in enumerate(sides):
            @pl.when(exists(-dg, -dt))
            def _():
                side_copy(i).wait_recv()
    for k in range(frames, 2 * frames):
        lay(k)
    for i, there in enumerate((has_up, has_down)):
        for k in range(frames):
            edge[i, k] = jnp.where(there, rims[i, frames + k], jnp.zeros((cols, ch), BF16))
    load_two.wait()
    add_edges(before, edge, frames, alone, hid, *args)
    for part in range(2):
        partial[part] = gather_taps(hid, frames - 1, w2, dims, part, (2, 1))

    def step(i, carry):
        f = frames - 1 - i
        arrive(f)
        spread(ext, hid, f, *args)
        for part in range(2):
            total = gather_taps(hid, f, w2, dims, part, (0,), partial[part])
            finish(total, ext, f, woven, stage, f - half, b2[...], length, frames, dims, part)
            partial[part] = gather_taps(hid, f - 1, w2, dims, part, (2, 1))
        return carry

    lax.fori_loop(0, half, step, 0)
    arrive(*reversed(range(half)))

    if comm:
        for i in range(2):
            @pl.when(exists(*sides[i]))
            def _():
                side_copy(i).wait_send()
        for f in range(frames):
            for i in range(3):
                @pl.when(exists(*onward[i]))
                def _():
                    onward_copy(i, f).wait_send()


def late_kernel(counts, comm, tile_rows, hid_late, ext, w1, w2, stage_late, partial, b1, b2, out, hid_early, stage, woven, out_sem):
    frames, cap, cols, ch = out.shape[0], out.shape[1] // 2, out.shape[2] // 2, out.shape[3]
    dims = (cap, cols, ch)
    half = frames // 2
    _, _, length, first, last = place_of(comm, counts, tile_rows)
    early, late = Frames(hid_early, 0), Frames(hid_late, half)
    hid = [early[k] if k < half else late[k] for k in range(frames + 2)]
    args = (w1, b1[...] * 0.5, first, last, length, dims)

    def out_copy(f):
        return pltpu.make_async_copy(stage_late.at[f - half], out.at[f], out_sem.at[f, 0])

    def half_copy(f, part):
        rows = slice(part * cap, (part + 1) * cap)
        return pltpu.make_async_copy(stage.at[f, rows], out.at[f, rows], out_sem.at[f, part])

    for f in range(half, frames):
        out_copy(f).start()
    for f in reversed(range(half)):
        spread(ext, hid, f, *args)
    for f in reversed(range(half)):
        for part in range(2):
            taps, rest = ((0,), partial[part]) if f == half - 1 else ((2, 1, 0), None)
            total = gather_taps(hid, f, w2, dims, part, taps, rest)
            finish(total, ext, f, woven, stage, f, b2[...], length, frames, dims, part)
            half_copy(f, part).start()
    for f in range(half, frames):
        out_copy(f).wait()
    for f in range(half):
        for part in range(2):
            half_copy(f, part).wait()


def run_block(counts, comm, latent, tile_rows, kernel_one, bias_one, kernel_two, bias_two):
    frames, cap, cols, ch = latent.shape
    half = frames // 2
    in_hbm = pl.BlockSpec(memory_space=pl.ANY)
    vmem = pl.BlockSpec(memory_space=pltpu.VMEM)
    smem = pl.BlockSpec(memory_space=pltpu.SMEM)
    dma = pltpu.SemaphoreType.DMA
    hidden = (4, cap + 1, 2, cols, ch)
    frame = (2 * cap, 2 * cols, ch)
    woven = (half, 2, 4 * cap * cols, ch // 2)
    bias_one, bias_two = bias_one.reshape(1, ch), bias_two.reshape(1, ch)
    kept = pl.pallas_call(
        functools.partial(early_kernel, counts, comm),
        out_shape=(
            pltpu.VMEM((frames + 2 - half, *hidden), BF16),
            pltpu.VMEM((2 * frames, (cap + 2) * cols, ch), BF16),
            pltpu.VMEM(kernel_one.shape, BF16),
            pltpu.VMEM(kernel_two.shape, BF16),
            pltpu.VMEM((half, *frame), BF16),
            pltpu.VMEM((2, 2 * cap * cols, ch), F32),
        ),
        in_specs=[smem, in_hbm, in_hbm, vmem, in_hbm, vmem],
        out_specs=[vmem] * 6,
        scratch_shapes=[
            pltpu.VMEM((frames, cap, cols, ch), BF16),
            pltpu.VMEM((2, 2 * frames, cols, ch), BF16),
            pltpu.VMEM((frames, cap, cols, ch), BF16),
            pltpu.VMEM((frames, cols, ch), BF16),
            pltpu.VMEM(woven, F32),
            pltpu.VMEM((2, frames, cols, ch), BF16),
            pltpu.VMEM((2, 2, 3, (cap + 1) * cols, ch), F32),
            dma((3,)), dma((2,)), dma((2,)), dma((3, frames)), dma((3, frames)),
        ],
        compiler_params=pltpu.CompilerParams(
            collective_id=0 if comm else None, has_side_effects=True, vmem_limit_bytes=44 * 2**20),
    )(tile_rows, latent, kernel_one, bias_one, kernel_two, bias_two)
    return pl.pallas_call(
        functools.partial(late_kernel, counts, comm),
        out_shape=jax.ShapeDtypeStruct((frames, *frame), BF16),
        in_specs=[smem] + [vmem] * 8,
        out_specs=in_hbm,
        scratch_shapes=[
            pltpu.VMEM((half, *hidden), BF16),
            pltpu.VMEM((half, *frame), BF16),
            pltpu.VMEM(woven, F32),
            dma((frames, 2)),
        ],
        compiler_params=pltpu.CompilerParams(vmem_limit_bytes=40 * 2**20),
    )(tile_rows, *kept, bias_one, bias_two)


def solution(mesh):
    counts = (mesh.shape["tm"], mesh.shape["tile"])
    in_specs = (P("tm", "tile", None, None), P(), P(), P(), P(), P())
    return jax.shard_map(functools.partial(run_block, counts, True), mesh=mesh, in_specs=in_specs,
                         out_specs=P("tm", "tile", None, None), check_vma=False)
```
